256 devices in a mesh: segment: 8 (over x, core), graph: 32 (over y, z).
Axes of the slice: x: 4, y: 4, z: 8, core: 2. Of those that a mesh axis runs over, the one named last changes fastest.
Arguments:
- state: float32 [8, 16384, 1024], P('segment', 'graph'), may hold values from -6 to 6
- initial: float32 [8, 16384, 1024], P('segment', 'graph'), may hold values from -6 to 6
- fresh: float32 [16384, 1024], P('graph'), may hold values from -6 to 6
- weights: float32 [8, 1024, 1024], P('segment'), may hold values from -0.1875 to 0.1875
- wants: int32 [32, 4, 1], P('graph'), may hold values from 0 to 3
- adj_slot: int32 [128, 4], P('graph'), may hold values from 0 to 7, as said below
- adj_count: int32 [128], P('graph'), may hold values from 2 to 4, as said below
- adj_vals: float32 [128, 4, 128, 128], P('graph'), may hold values from -0.25 to 0.25
Outputs:
- handed: float32 [8, 16384, 1024], P('segment', 'graph')
- advanced: float32 [8, 16384, 1024], P('segment', 'graph')
The draws below stay inside these ranges and needn't reach their ends.
Inputs may be any that keep to these rules, and one draw needn't show every extreme that they name: `adj_slot`: every entry of a destination block's row at k < 2 names a slot past the partition's own blocks, and every such slot of a partition is named at some k < 2 of one of its blocks. `adj_count`: each partition has a block with exactly 4 nonzero blocks.
All inputs are finite; a program needn't handle non-finite values.
Results may differ from the reference program's by a relative error of at most 0.0001.
Values sent between devices are 32-bit elements; how exact they have to be, the bound alone decides.
A program may use at most 128 MiB of HBM per device.

```python
import jax
import jax.numpy as jnp
from jax import lax

D = 1024
BLK = 128
V_DEV = 512
KMAX = 4
REACH = 2
CAP = 1
NB = 4
VBLK = 128
N = 16384
N_SEGMENT = 8
N_GRAPH = 32


def draw_adj_slot(key, part):
    key_base = jax.random.fold_in(key, 11)
    key_shift = jax.random.fold_in(key, 12)
    received_count = 2 * REACH * CAP
    base = jax.random.randint(key_base, (N_GRAPH, NB, KMAX), 0, NB + received_count).astype(jnp.int32)
    rotation = jax.random.randint(key_shift, (N_GRAPH, 1), 0, received_count).astype(jnp.int32)
    positions = jnp.arange(2 * NB, dtype=jnp.int32)[None, :]
    forced = NB + (positions + rotation) % received_count
    forced = forced.reshape(N_GRAPH, NB, 2)
    merged = jnp.concatenate([forced, base[:, :, 2:]], axis=2)
    return merged.reshape(VBLK, KMAX).astype(jnp.int32)


def draw_adj_count(key, part):
    key_base = jax.random.fold_in(key, 21)
    key_row = jax.random.fold_in(key, 22)
    counts = jax.random.randint(key_base, (N_GRAPH, NB), 2, KMAX + 1).astype(jnp.int32)
    chosen_row = jax.random.randint(key_row, (N_GRAPH, 1), 0, NB).astype(jnp.int32)
    columns = jnp.arange(NB, dtype=jnp.int32)[None, :]
    counts = jnp.where(columns == chosen_row, KMAX, counts)
    return counts.reshape(VBLK).astype(jnp.int32)


def with_ends(result, own_key, smallest, top_value):
    longest = result.shape.index(max(result.shape))
    spots = []
    for shift in (0, 1):
        where = [jax.random.randint(jax.random.fold_in(own_key, axis), (), 0, length) for axis, length in enumerate(result.shape)]
        where[longest] = (where[longest] + shift) % result.shape[longest]
        spots.append(tuple(where))
    return result.at[spots[0]].set(smallest).at[spots[1]].set(top_value)


def level_of(stream_key, extent, cuts, least, top_value):
    factor_of = 1.0
    for dim, blocks in cuts:
        steps = jax.random.uniform(jax.random.fold_in(jax.random.fold_in(stream_key, 6), dim), (blocks,), jnp.float32, least / len(cuts), top_value / len(cuts))
        factor_of = factor_of * jnp.repeat(jnp.exp(steps), extent[dim] // blocks).reshape((-1,) + (1,) * (len(extent) - 1 - dim))
    return factor_of


def bell_draw(stream_key, extent, width, bound, pieces=(), kind=jnp.bfloat16):
    result = width * jax.random.normal(stream_key, extent, jnp.float32)
    if pieces:
        result = result * level_of(stream_key, extent, pieces, -0.22, 0.18)
    return jnp.clip(result, -bound, bound).astype(kind)


def setup_inputs(seed: int = 0) -> dict:
    splits = jax.random.split(jax.random.key(seed), 9)
    return {
        "state": bell_draw(splits[0], (N_SEGMENT, N, D), 1.0, 6.0, ((0, 8), (1, 32)), jnp.float32),
        "initial": bell_draw(splits[1], (N_SEGMENT, N, D), 1.0, 6.0, ((0, 8), (1, 32)), jnp.float32),
        "fresh": bell_draw(splits[2], (N, D), 1.0, 6.0, ((0, 32),), jnp.float32),
        "weights": bell_draw(splits[3], (N_SEGMENT, D, D), D ** -0.5, 0.1875, ((0, 8),), jnp.float32),
        "wants": with_ends(jax.random.randint(splits[4], (N_GRAPH, 2 * REACH, CAP), 0, NB), jax.random.fold_in(splits[4], 1), 0, NB - 1).astype(jnp.int32),
        "adj_slot": draw_adj_slot(jax.random.fold_in(splits[8], 71), 0),
        "adj_count": draw_adj_count(jax.random.fold_in(splits[8], 71), 0),
        "adj_vals": bell_draw(splits[7], (VBLK, KMAX, BLK, BLK), (BLK * KMAX) ** -0.5, 0.25, ((0, 32),), jnp.float32),
    }


def offset_list():
    found = []
    for radius in range(1, REACH + 1):
        found.append(radius)
        found.append(-radius)
    return found


def apply_layer(feats, first_feats, weight, layer_index, wants, adj_slot, adj_count, adj_vals):
    parts = N_GRAPH
    nblocks = V_DEV // BLK
    row_blocks = feats.reshape(parts, nblocks, BLK, D)
    partition = jnp.arange(parts, dtype=jnp.int32)
    received = []
    for position, shift_by in enumerate(offset_list()):
        source = partition - shift_by
        valid = ((source >= 0) & (source < parts)).astype(jnp.float32)
        clipped = jnp.clip(source, 0, parts - 1).astype(jnp.int32)
        chosen = wants[:, position, :]
        picked = row_blocks[clipped[:, None], chosen]
        received.append(picked * valid[:, None, None, None])
    sources = jnp.concatenate([row_blocks] + received, axis=1)
    slots = adj_slot.reshape(parts, nblocks, KMAX)
    selected = sources[partition[:, None, None], slots]
    live = (jnp.arange(KMAX, dtype=jnp.int32)[None, None, :] < adj_count.reshape(parts, nblocks)[:, :, None]).astype(jnp.float32)
    values = adj_vals.reshape(parts, nblocks, KMAX, BLK, BLK) * live[:, :, :, None, None]
    agg = jnp.einsum("gbkij,gbkjd->gbid", values, selected, precision=lax.Precision.HIGHEST).reshape(parts * nblocks * BLK, D)
    mixed = 0.9 * agg + 0.1 * first_feats
    beta = jnp.log(0.5 / (layer_index + 1.0) + 1.0)
    product = jnp.dot(mixed, weight, precision=lax.Precision.HIGHEST, preferred_element_type=jnp.float32)
    return jax.nn.relu((1.0 - beta) * mixed + beta * product)


def reference(state, initial, fresh, weights, wants, adj_slot, adj_count, adj_vals):
    handed_list = []
    for section in range(N_SEGMENT):
        handed_list.append(apply_layer(state[section], initial[section], weights[section], float(section), wants, adj_slot, adj_count, adj_vals))
    advanced_list = []
    for section in range(N_SEGMENT):
        if section == 0:
            feats, first_feats = fresh, fresh
        else:
            feats, first_feats = handed_list[section - 1], initial[section - 1]
        advanced_list.append(apply_layer(feats, first_feats, weights[section], float(section), wants, adj_slot, adj_count, adj_vals))
    return jnp.stack(handed_list), jnp.stack(advanced_list)
```

```python
import functools
import math

import jax
import jax.numpy as jnp
from jax import lax
from jax.experimental import pallas as pl
from jax.experimental.pallas import tpu as pltpu
from jax.sharding import PartitionSpec as P

MESH = pl.DeviceIdType.MESH
F32 = jnp.float32
BF16 = jnp.bfloat16
D = 1024
BLK = 128
NB = 4
KMAX = 4
V = NB * BLK
OFFSETS = (1, -1, 2, -2)
NJ = len(OFFSETS)
NC = 4
CW = D // NC
ORDER = (2, 3, 0, 1)


def split(x):
    hi = x.astype(BF16)
    return hi, (x - hi.astype(F32)).astype(BF16)


def dot(a, b):
    return jnp.dot(a, b, preferred_element_type=F32)


def kernel(
    n_seg, n_graph,
    slot, count, state, initial, fresh, weights, vals, wants,
    handed, advanced,
    state_v, vals_v, w_v, init_v, init_in, stage1, stage2, recv1, recv2,
    a_hi, a_lo, w_hi, w_lo, z, acc, out2, wants_in, *rest,
):
    h_in, h_out = rest[:NC], rest[NC : 2 * NC]
    (load_sem, want_send, want_recv, z_send, z_recv, x_send, h_recv, init_sem, init_recv, out_sem, adv_sem) = rest[2 * NC :]
    sec = lax.axis_index("segment")
    part = lax.axis_index("graph")
    first, last = sec == 0, sec == n_seg - 1
    dests = [part + o for o in OFFSETS]
    sources = [part - o for o in OFFSETS]
    has_dest = [(d >= 0) & (d < n_graph) for d in dests]
    has_source = [(d >= 0) & (d < n_graph) for d in sources]

    def cols(c):
        return pl.ds(c * CW, CW)

    loads = [
        pltpu.make_async_copy(src, dst, load_sem.at[i])
        for i, (src, dst) in enumerate(
            ((state, state_v), (vals, vals_v), (weights, w_v), (initial, init_v))
        )
    ]
    for load in loads:
        load.start()

    barrier = pltpu.get_barrier_semaphore()
    expected = jnp.int32(0)
    for d, ok in zip(dests, has_dest):
        @pl.when(ok)
        def _():
            pl.semaphore_signal(barrier, inc=1, device_id={"graph": d}, device_id_type=MESH)
        expected += ok.astype(jnp.int32)

    @pl.when(jnp.logical_not(last))
    def _():
        pl.semaphore_signal(barrier, inc=1, device_id={"segment": sec + 1}, device_id_type=MESH)

    @pl.when(jnp.logical_not(first))
    def _():
        pl.semaphore_signal(barrier, inc=1, device_id={"segment": sec - 1}, device_id_type=MESH)

    expected += jnp.logical_not(last).astype(jnp.int32) + jnp.logical_not(first).astype(jnp.int32)
    pl.semaphore_wait(barrier, expected)

    def want_copy(j):
        return pltpu.make_async_remote_copy(
            src_ref=wants, dst_ref=wants_in.at[j], send_sem=want_send.at[j], recv_sem=want_recv.at[j],
            device_id={"graph": sources[j]}, device_id_type=MESH,
        )

    def init_copy():
        return pltpu.make_async_remote_copy(
            src_ref=initial, dst_ref=init_in, send_sem=init_sem, recv_sem=init_recv,
            device_id={"segment": sec + 1}, device_id_type=MESH,
        )

    for j in ORDER:
        @pl.when(has_source[j])
        def _():
            want_copy(j).start()

    @pl.when(jnp.logical_not(last))
    def _():
        init_copy().start()

    @pl.when(first)
    def _():
        pltpu.make_async_copy(fresh, init_in, init_recv).start()
        for c in range(NC):
            pltpu.make_async_copy(fresh.at[:, :, cols(c)], h_in[c], h_recv.at[c]).start()

    loads[1].wait()

    def build(b, carry):
        for s in range(NB + NJ):
            tile = jnp.zeros((BLK, BLK), F32)
            for k in range(KMAX):
                live = ((slot[b, k] == s) & (k < count[b])).astype(jnp.int32)
                tile += live.astype(F32) * vals_v[b, k]
            hi, lo = split(0.9 * tile)
            rows = pl.ds(pl.multiple_of(b * BLK, BLK), BLK)
            a_hi[rows, pl.ds(s * BLK, BLK)] = hi
            a_lo[rows, pl.ds(s * BLK, BLK)] = lo
        return carry

    lax.fori_loop(0, NB, build, 0)

    loads[0].wait()
    for j in ORDER:
        @pl.when(has_dest[j])
        def _():
            want_copy(j).wait_recv()

        @pl.when(jnp.logical_not(has_source[j]))
        def _():
            recv1[j] = jnp.zeros((NC, BLK, CW), F32)
            recv2[j] = jnp.zeros((NC, BLK, CW), F32)

    def block_copy(tick, j, c):
        return pltpu.make_async_remote_copy(
            src_ref=(stage1, stage2)[tick].at[j, c], dst_ref=(recv1, recv2)[tick].at[j, c],
            send_sem=z_send.at[tick, j, c], recv_sem=z_recv.at[tick, j, c],
            device_id={"graph": dests[j]}, device_id_type=MESH,
        )

    def send_blocks(tick, c):
        for j in ORDER:
            @pl.when(has_dest[j])
            def _():
                block = wants_in[j, j]
                if tick == 0:
                    stage1[j, c] = state_v[block, :, cols(c)]
                else:
                    stage2[j, c] = h_in[c][block]
                block_copy(tick, j, c).start()

    for c in range(NC):
        send_blocks(0, c)

    beta = jnp.float32(0.0)
    for s in range(n_seg):
        beta = jnp.where(sec == s, jnp.float32(math.log(0.5 / (s + 1.0) + 1.0)), beta)
    loads[2].wait()

    def fold(i, carry):
        rows = pl.ds(pl.multiple_of(i * BLK, BLK), BLK)
        r = lax.broadcasted_iota(jnp.int32, (BLK, D), 0) + i * BLK
        q = lax.broadcasted_iota(jnp.int32, (BLK, D), 1)
        w = beta * w_v[rows, :] + jnp.where(r == q, 1.0 - beta, 0.0)
        w_hi[rows, :], w_lo[rows, :] = split(w)
        return carry

    lax.fori_loop(0, D // BLK, fold, 0)

    def aggregate(lo_col, feats):
        hi, lo = split(feats)
        k = pl.ds(lo_col, NB * BLK)
        return dot(a_hi[:, k], hi) + dot(a_lo[:, k], hi) + dot(a_hi[:, k], lo)

    def own_part(feats, first_feats, c):
        z[c] = aggregate(0, feats) + 0.1 * first_feats

    def rest_part(tick, c, finish):
        for j in ORDER:
            @pl.when(has_source[j])
            def _():
                block_copy(tick, j, c).wait_recv()
        recv = (recv1, recv2)[tick]
        zc = z[c] + aggregate(V, recv[:, c].reshape(V, CW))
        hi, lo = split(zc)
        for n in range(NC):
            part_n = dot(hi, w_hi[cols(c), cols(n)]) + dot(lo, w_hi[cols(c), cols(n)]) + dot(hi, w_lo[cols(c), cols(n)])
            if c > 0:
                part_n += acc[n]
            if c < NC - 1:
                acc[n] = part_n
            else:
                finish(n, jnp.maximum(part_n, 0.0))

    loads[3].wait()
    for c in range(NC):
        own_part(state_v[:, :, cols(c)].reshape(V, CW), init_v[:, :, cols(c)].reshape(V, CW), c)

    def hand_copy(n):
        return pltpu.make_async_remote_copy(
            src_ref=h_out[n], dst_ref=h_in[n], send_sem=x_send.at[n], recv_sem=h_recv.at[n],
            device_id={"segment": sec + 1}, device_id_type=MESH,
        )

    def hand_store(n):
        return pltpu.make_async_copy(h_out[n], handed.at[:, :, cols(n)], out_sem.at[n])

    def finish_first(n, value):
        h_out[n][...] = value.reshape(NB, BLK, CW)

        @pl.when(jnp.logical_not(last))
        def _():
            hand_copy(n).start()
        hand_store(n).start()

    for c in range(NC):
        rest_part(0, c, finish_first)

    def take(c):
        pltpu.make_async_copy(h_in[c], h_in[c], h_recv.at[c]).wait()
        send_blocks(1, c)
        if c == 0:
            pltpu.make_async_copy(init_in, init_in, init_recv).wait()
        own_part(h_in[c][...].reshape(V, CW), init_in[:, :, cols(c)].reshape(V, CW), c)

    def adv_store(n):
        return pltpu.make_async_copy(out2.at[n], advanced.at[:, :, cols(n)], adv_sem.at[n])

    def finish_second(n, value):
        out2[n] = value.reshape(NB, BLK, CW)
        adv_store(n).start()

    take(0)
    for c in range(NC):
        if c + 1 < NC:
            take(c + 1)
        rest_part(1, c, finish_second)

    for j in range(NJ):
        @pl.when(has_source[j])
        def _():
            want_copy(j).wait_send()

        @pl.when(has_dest[j])
        def _():
            for tick in range(2):
                for c in range(NC):
                    block_copy(tick, j, c).wait_send()

    @pl.when(jnp.logical_not(last))
    def _():
        init_copy().wait_send()
        for n in range(NC):
            hand_copy(n).wait_send()

    for n in range(NC):
        hand_store(n).wait()
        adv_store(n).wait()


def blocks(x):
    return x.reshape(NB, BLK, D)


def shards(n_seg, n_graph, state, initial, fresh, weights, wants, adj_slot, adj_count, adj_vals):
    smem = pl.BlockSpec(memory_space=pltpu.SMEM)
    hbm = pl.BlockSpec(memory_space=pl.ANY)
    out = jax.ShapeDtypeStruct((NB, BLK, D), F32)
    dma = pltpu.SemaphoreType.DMA
    handed, advanced = pl.pallas_call(
        functools.partial(kernel, n_seg, n_graph),
        out_shape=(out, out),
        in_specs=[smem, smem] + [hbm] * 5 + [smem],
        out_specs=(hbm, hbm),
        scratch_shapes=[
            pltpu.VMEM((NB, BLK, D), F32),
            pltpu.VMEM((NB, KMAX, BLK, BLK), F32),
            pltpu.VMEM((D, D), F32),
            pltpu.VMEM((NB, BLK, D), F32),
            pltpu.VMEM((NB, BLK, D), F32),
            pltpu.VMEM((NJ, NC, BLK, CW), F32),
            pltpu.VMEM((NJ, NC, BLK, CW), F32),
            pltpu.VMEM((NJ, NC, BLK, CW), F32),
            pltpu.VMEM((NJ, NC, BLK, CW), F32),
            pltpu.VMEM((V, (NB + NJ) * BLK), BF16),
            pltpu.VMEM((V, (NB + NJ) * BLK), BF16),
            pltpu.VMEM((D, D), BF16),
            pltpu.VMEM((D, D), BF16),
            pltpu.VMEM((NC, V, CW), F32),
            pltpu.VMEM((NC, V, CW), F32),
            pltpu.VMEM((NC, NB, BLK, CW), F32),
            pltpu.SMEM((NJ, NJ), jnp.int32),
        ]
        + [pltpu.VMEM((NB, BLK, CW), F32) for _ in range(2 * NC)]
        + [
            dma((4,)), dma((NJ,)), dma((NJ,)), dma((2, NJ, NC)), dma((2, NJ, NC)),
            dma((NC,)), dma((NC,)), dma, dma, dma((NC,)), dma((NC,)),
        ],
        compiler_params=pltpu.CompilerParams(
            collective_id=0, has_side_effects=True, vmem_limit_bytes=60 * 1024 * 1024
        ),
    )(
        adj_slot, adj_count, blocks(state), blocks(initial), blocks(fresh), weights[0], adj_vals, wants.reshape(NJ)
    )
    return handed.reshape(1, V, D), advanced.reshape(1, V, D)


def solution(mesh):
    return jax.shard_map(
        functools.partial(shards, mesh.shape["segment"], mesh.shape["graph"]),
        mesh=mesh,
        in_specs=(
            P("segment", "graph", None),
            P("segment", "graph", None),
            P("graph", None),
            P("segment", None, None),
            P("graph", None, None),
            P("graph", None),
            P("graph"),
            P("graph", None, None, None),
        ),
        out_specs=(P("segment", "graph", None), P("segment", "graph", None)),
        check_vma=False,
    )
```

```python
import functools
import math

import jax
import jax.numpy as jnp
from jax import lax
from jax.experimental import pallas as pl
from jax.experimental.pallas import tpu as pltpu
from jax.sharding import PartitionSpec as P

MESH = pl.DeviceIdType.MESH
F32 = jnp.float32
BF16 = jnp.bfloat16
D = 1024
BLK = 128
NB = 4
KMAX = 4
V = NB * BLK
OFFSETS = (1, -1, 2, -2)
NJ = len(OFFSETS)
WIDTHS = (256, 256, 256, 128, 128)
NC = len(WIDTHS)
STARTS = tuple(sum(WIDTHS[:c]) for c in range(NC))
ORDER = (2, 3, 0, 1)
GO = 2


def split(x):
    hi = x.astype(BF16)
    return hi, (x - hi.astype(F32)).astype(BF16)


def dot(a, b):
    return jnp.dot(a, b, preferred_element_type=F32)


def kernel(
    n_seg, n_graph,
    slot_hbm, count_hbm, state, initial, fresh, weights, vals, wants_hbm,
    handed, advanced,
    state_v, vals_v, w_v, init_v, init_in,
    a_hi, a_lo, w_hi, w_lo, wants_in, slot, count, *rest,
):
    h_in, stage1, stage2, recv1, recv2, z, acc = (rest[i * NC : (i + 1) * NC] for i in range(7))
    (load_sem, want_send, want_recv, z_send, z_recv, x_send, h_recv, init_sem, init_recv, go_sem) = rest[7 * NC :]
    sec = lax.axis_index("segment")
    part = lax.axis_index("graph")
    first, last = sec == 0, sec == n_seg - 1
    odd = sec % 2 == 1
    dests = [part + o for o in OFFSETS]
    sources = [part - o for o in OFFSETS]
    has_dest = [(d >= 0) & (d < n_graph) for d in dests]
    has_source = [(d >= 0) & (d < n_graph) for d in sources]

    def cols(c):
        return pl.ds(STARTS[c], WIDTHS[c])

    loads = [
        pltpu.make_async_copy(src, dst, load_sem.at[i])
        for i, (src, dst) in enumerate(
            ((state, state_v), (vals, vals_v), (weights, w_v), (initial, init_v), (slot_hbm, slot), (count_hbm, count))
        )
    ]
    loads[0].start()

    barrier = pltpu.get_barrier_semaphore()
    expected = jnp.int32(0)
    for d, ok in zip(dests, has_dest):
        @pl.when(ok)
        def _():
            pl.semaphore_signal(barrier, inc=1, device_id={"graph": d}, device_id_type=MESH)
        expected += ok.astype(jnp.int32)

    @pl.when(jnp.logical_not(last))
    def _():
        pl.semaphore_signal(barrier, inc=1, device_id={"segment": sec + 1}, device_id_type=MESH)

    @pl.when(jnp.logical_not(first))
    def _():
        pl.semaphore_signal(barrier, inc=1, device_id={"segment": sec - 1}, device_id_type=MESH)

    expected += jnp.logical_not(last).astype(jnp.int32) + jnp.logical_not(first).astype(jnp.int32)
    pl.semaphore_wait(barrier, expected)

    def want_copy(j):
        return pltpu.make_async_remote_copy(
            src_ref=wants_hbm, dst_ref=wants_in.at[j], send_sem=want_send.at[j], recv_sem=want_recv.at[j],
            device_id={"graph": sources[j]}, device_id_type=MESH,
        )

    def init_copy():
        return pltpu.make_async_remote_copy(
            src_ref=initial, dst_ref=init_in, send_sem=init_sem, recv_sem=init_recv,
            device_id={"segment": sec + 1}, device_id_type=MESH,
        )

    for j in ORDER:
        @pl.when(has_source[j])
        def _():
            want_copy(j).start()

    for load in loads[1:]:
        load.start()

    @pl.when(jnp.logical_not(last))
    def _():
        init_copy().start()

    @pl.when(first)
    def _():
        pltpu.make_async_copy(fresh, init_in, init_recv).start()
        for c in range(NC):
            pltpu.make_async_copy(fresh.at[:, :, cols(c)], h_in[c], h_recv.at[c]).start()

    def block_copy(tick, j, c):
        return pltpu.make_async_remote_copy(
            src_ref=(stage1, stage2)[tick][c].at[j], dst_ref=(recv1, recv2)[tick][c].at[j],
            send_sem=z_send.at[tick, j, c], recv_sem=z_recv.at[tick, j, c],
            device_id={"graph": dests[j]}, device_id_type=MESH,
        )

    loads[0].wait()
    for c in range(NC):
        for j in ORDER:
            @pl.when(has_dest[j])
            def _():
                if c == 0:
                    want_copy(j).wait_recv()
                stage1[c][j] = state_v[wants_in[j, j], :, cols(c)]

                @pl.when(odd)
                def _():
                    block_copy(0, j, c).start()

    for j in ORDER:
        @pl.when(jnp.logical_not(has_source[j]))
        def _():
            for c in range(NC):
                recv1[c][j] = jnp.zeros((BLK, WIDTHS[c]), F32)
                recv2[c][j] = jnp.zeros((BLK, WIDTHS[c]), F32)

    loads[1].wait()
    loads[4].wait()
    loads[5].wait()

    def build(b, carry):
        for s in range(NB + NJ):
            tile = jnp.zeros((BLK, BLK), F32)
            for k in range(KMAX):
                live = ((slot[b, k] == s) & (k < count[b])).astype(jnp.int32)
                tile += live.astype(F32) * vals_v[b, k]
            hi, lo = split(0.9 * tile)
            rows = pl.ds(pl.multiple_of(b * BLK, BLK), BLK)
            a_hi[rows, pl.ds(s * BLK, BLK)] = hi
            a_lo[rows, pl.ds(s * BLK, BLK)] = lo
        return carry

    lax.fori_loop(0, NB, build, 0)

    beta = jnp.float32(0.0)
    for s in range(n_seg):
        beta = jnp.where(sec == s, jnp.float32(math.log(0.5 / (s + 1.0) + 1.0)), beta)
    loads[2].wait()

    def fold(i, carry):
        rows = pl.ds(pl.multiple_of(i * BLK, BLK), BLK)
        r = lax.broadcasted_iota(jnp.int32, (BLK, D), 0) + i * BLK
        q = lax.broadcasted_iota(jnp.int32, (BLK, D), 1)
        w = beta * w_v[rows, :] + jnp.where(r == q, 1.0 - beta, 0.0)
        w_hi[rows, :], w_lo[rows, :] = split(w)
        return carry

    lax.fori_loop(0, D // BLK, fold, 0)

    def aggregate(lo_col, feats):
        hi, lo = split(feats)
        k = pl.ds(lo_col, NB * BLK)
        return dot(a_hi[:, k], hi) + dot(a_lo[:, k], hi) + dot(a_hi[:, k], lo)

    def own_part(feats, first_feats, c):
        z[c][...] = aggregate(0, feats) + 0.1 * first_feats

    def rest_part(tick, c, finish):
        for j in ORDER:
            @pl.when(has_source[j])
            def _():
                block_copy(tick, j, c).wait_recv()
        recv = (recv1, recv2)[tick][c]
        if tick == 0 and c == GO:
            @pl.when(odd)
            def _():
                pl.semaphore_signal(go_sem, inc=1, device_id={"segment": sec - 1}, device_id_type=MESH)
        zc = z[c][...] + aggregate(V, recv[...].reshape(V, WIDTHS[c]))
        hi, lo = split(zc)
        for n in range(NC):
            part_n = dot(hi, w_hi[cols(c), cols(n)]) + dot(lo, w_hi[cols(c), cols(n)]) + dot(hi, w_lo[cols(c), cols(n)])
            if c > 0:
                part_n += acc[n][...]
            if c < NC - 1:
                acc[n][...] = part_n
            else:
                finish(n, jnp.maximum(part_n, 0.0))

    loads[3].wait()
    for c in range(NC):
        own_part(state_v[:, :, cols(c)].reshape(V, WIDTHS[c]), init_v[:, :, cols(c)].reshape(V, WIDTHS[c]), c)

    def hand_copy(n):
        return pltpu.make_async_remote_copy(
            src_ref=handed.at[:, :, cols(n)], dst_ref=h_in[n], send_sem=x_send.at[n], recv_sem=h_recv.at[n],
            device_id={"segment": sec + 1}, device_id_type=MESH,
        )

    def finish_first(n, value):
        handed[:, :, cols(n)] = value.reshape(NB, BLK, WIDTHS[n])

        @pl.when(jnp.logical_not(last))
        def _():
            hand_copy(n).start()

    @pl.when(jnp.logical_not(odd))
    def _():
        pl.semaphore_wait(go_sem, 1)
        for c in range(NC):
            for j in ORDER:
                @pl.when(has_dest[j])
                def _():
                    block_copy(0, j, c).start()

    def forward(c):
        pltpu.make_async_copy(h_in[c], h_in[c], h_recv.at[c]).wait()
        for j in ORDER:
            @pl.when(has_dest[j])
            def _():
                stage2[c][j] = h_in[c][wants_in[j, j]]
                block_copy(1, j, c).start()

    def early(c):
        @pl.when(jnp.logical_not(odd))
        def _():
            forward(c)

    for c in range(NC):
        rest_part(0, c, finish_first)
        if c == 0:
            early(0)
        if c == 2:
            early(1)

    @pl.when(odd)
    def _():
        forward(0)
        forward(1)
    for c in range(2, NC):
        forward(c)

    def finish_second(n, value):
        advanced[:, :, cols(n)] = value.reshape(NB, BLK, WIDTHS[n])

    pltpu.make_async_copy(init_in, init_in, init_recv).wait()
    for c in range(NC):
        own_part(h_in[c][...].reshape(V, WIDTHS[c]), init_in[:, :, cols(c)].reshape(V, WIDTHS[c]), c)
    for c in range(NC):
        rest_part(1, c, finish_second)

    for j in range(NJ):
        @pl.when(has_source[j])
        def _():
            want_copy(j).wait_send()

        @pl.when(has_dest[j])
        def _():
            for tick in range(2):
                for c in range(NC):
                    block_copy(tick, j, c).wait_send()

    @pl.when(jnp.logical_not(last))
    def _():
        init_copy().wait_send()
        for n in range(NC):
            hand_copy(n).wait_send()


def blocks(x):
    return x.reshape(NB, BLK, D)


def shards(n_seg, n_graph, state, initial, fresh, weights, wants, adj_slot, adj_count, adj_vals):
    smem = pl.BlockSpec(memory_space=pltpu.SMEM)
    hbm = pl.BlockSpec(memory_space=pltpu.HBM)
    vmem = pl.BlockSpec(memory_space=pltpu.VMEM)
    out = jax.ShapeDtypeStruct((NB, BLK, D), F32)
    dma = pltpu.SemaphoreType.DMA
    handed, advanced = pl.pallas_call(
        functools.partial(kernel, n_seg, n_graph),
        out_shape=(out, out),
        in_specs=[hbm] * 8,
        out_specs=(vmem, vmem),
        scratch_shapes=[
            pltpu.VMEM((NB, BLK, D), F32),
            pltpu.VMEM((NB, KMAX, BLK, BLK), F32),
            pltpu.VMEM((D, D), F32),
            pltpu.VMEM((NB, BLK, D), F32),
            pltpu.VMEM((NB, BLK, D), F32),
            pltpu.VMEM((V, (NB + NJ) * BLK), BF16),
            pltpu.VMEM((V, (NB + NJ) * BLK), BF16),
            pltpu.VMEM((D, D), BF16),
            pltpu.VMEM((D, D), BF16),
            pltpu.SMEM((NJ, NJ), jnp.int32),
            pltpu.SMEM((NB, KMAX), jnp.int32),
            pltpu.SMEM((NB,), jnp.int32),
        ]
        + [pltpu.VMEM((NB, BLK, w), F32) for _ in range(5) for w in WIDTHS]
        + [pltpu.VMEM((V, w), F32) for _ in range(2) for w in WIDTHS]
        + [
            dma((6,)), dma((NJ,)), dma((NJ,)), dma((2, NJ, NC)), dma((2, NJ, NC)),
            dma((NC,)), dma((NC,)), dma, dma,
            pltpu.SemaphoreType.REGULAR,
        ],
        compiler_params=pltpu.CompilerParams(
            collective_id=0, has_side_effects=True, vmem_limit_bytes=48 * 1024 * 1024
        ),
    )(
        *(
            pltpu.with_memory_space_constraint(x, pltpu.HBM)
            for x in (
                adj_slot, adj_count, blocks(state), blocks(initial), blocks(fresh), weights[0], adj_vals,
                wants.reshape(NJ),
            )
        )
    )
    return handed.reshape(1, V, D), advanced.reshape(1, V, D)


def solution(mesh):
    return jax.shard_map(
        functools.partial(shards, mesh.shape["segment"], mesh.shape["graph"]),
        mesh=mesh,
        in_specs=(
            P("segment", "graph", None),
            P("segment", "graph", None),
            P("graph", None),
            P("segment", None, None),
            P("graph", None, None),
            P("graph", None),
            P("graph"),
            P("graph", None, None, None),
        ),
        out_specs=(P("segment", "graph", None), P("segment", "graph", None)),
        check_vma=False,
    )
```

```python
import functools
import math

import jax
import jax.numpy as jnp
from jax import lax
from jax.experimental import pallas as pl
from jax.experimental.pallas import tpu as pltpu
from jax.sharding import PartitionSpec as P

MESH = pl.DeviceIdType.MESH
F32 = jnp.float32
BF16 = jnp.bfloat16
D = 1024
BLK = 128
NB = 4
KMAX = 4
V = NB * BLK
OFFSETS = (1, -1, 2, -2)
NJ = len(OFFSETS)
WIDTHS = (256, 256, 256, 128, 128)
NC = len(WIDTHS)
STARTS = tuple(sum(WIDTHS[:c]) for c in range(NC))
ORDER = (0, 1, 2, 3)
GO = 2


def split(x):
    hi = x.astype(BF16)
    return hi, (x - hi.astype(F32)).astype(BF16)


def dot(a, b):
    return jnp.dot(a, b, preferred_element_type=F32)


def adjacent(a_hi, a_lo, feats):
    hi, lo = split(feats)
    width = feats.shape[1]
    if width > BLK:
        return dot(a_hi, hi) + dot(a_lo, hi) + dot(a_hi, lo)
    both = dot(a_hi, jnp.concatenate([hi, lo], axis=1))
    return both[:, :width] + both[:, width:] + dot(a_lo, hi)


def weighted(parts, w_hi, w_lo):
    hi, lo = parts
    if hi.shape[1] > BLK:
        return dot(hi, w_hi) + dot(lo, w_hi) + dot(hi, w_lo)
    return dot(jnp.concatenate([hi, lo], axis=1), jnp.concatenate([w_hi, w_hi], axis=0)) + dot(hi, w_lo)


def cols(c):
    return pl.ds(STARTS[c], WIDTHS[c])


def kernel(
    n_seg, n_graph,
    slot_hbm, count_hbm, state, initial, fresh, weights, vals, wants_hbm,
    handed, acc, z_last, recv_last, a_hi, a_lo, w_hi, w_lo,
    state_v, vals_v, w_v, init_v, init_in, wants_in, slot, count, *rest,
):
    h_in, stage1, stage2, recv1, recv2, z = (rest[i * NC : (i + 1) * NC] for i in range(6))
    recv2 = recv2[: NC - 1] + (recv_last,)
    (load_sem, want_send, want_recv, z_send, z_recv, x_send, h_recv, init_recv, go_sem) = rest[6 * NC :]
    sec = lax.axis_index("segment")
    part = lax.axis_index("graph")
    first, last = sec == 0, sec == n_seg - 1
    odd = sec % 2 == 1
    dests = [part + o for o in OFFSETS]
    sources = [part - o for o in OFFSETS]
    has_dest = [(d >= 0) & (d < n_graph) for d in dests]
    has_source = [(d >= 0) & (d < n_graph) for d in sources]

    due = sum(ok.astype(jnp.int32) for ok in has_source)

    loads = [
        pltpu.make_async_copy(src, dst, load_sem.at[i])
        for i, (src, dst) in enumerate(
            ((state, state_v), (vals, vals_v), (weights, w_v), (initial, init_v), (slot_hbm, slot), (count_hbm, count))
        )
    ]
    loads[0].start()

    barrier = pltpu.get_barrier_semaphore()
    expected = jnp.int32(0)
    for d, ok in zip(dests, has_dest):
        @pl.when(ok)
        def _():
            pl.semaphore_signal(barrier, inc=1, device_id={"graph": d}, device_id_type=MESH)
        expected += ok.astype(jnp.int32)

    @pl.when(jnp.logical_not(last))
    def _():
        pl.semaphore_signal(barrier, inc=1, device_id={"segment": sec + 1}, device_id_type=MESH)

    @pl.when(jnp.logical_not(first))
    def _():
        pl.semaphore_signal(barrier, inc=1, device_id={"segment": sec - 1}, device_id_type=MESH)

    expected += jnp.logical_not(last).astype(jnp.int32) + jnp.logical_not(first).astype(jnp.int32)
    pl.semaphore_wait(barrier, expected)

    def want_copy(j):
        return pltpu.make_async_remote_copy(
            src_ref=wants_hbm, dst_ref=wants_in.at[j], send_sem=want_send.at[j], recv_sem=want_recv.at[j],
            device_id={"graph": sources[j]}, device_id_type=MESH,
        )

    def init_copy():
        return pltpu.make_async_remote_copy(
            src_ref=initial, dst_ref=init_in, send_sem=x_send, recv_sem=init_recv,
            device_id={"segment": sec + 1}, device_id_type=MESH,
        )

    for j in ORDER:
        @pl.when(has_source[j])
        def _():
            want_copy(j).start()

    for load in loads[1:]:
        load.start()

    @pl.when(jnp.logical_not(last))
    def _():
        init_copy().start()

    @pl.when(first)
    def _():
        pltpu.make_async_copy(fresh, init_in, init_recv).start()
        for c in range(NC):
            pltpu.make_async_copy(fresh.at[:, :, cols(c)], h_in[c], h_recv.at[c]).start()

    def block_copy(tick, j, c):
        return pltpu.make_async_remote_copy(
            src_ref=(stage1, stage2)[tick][c].at[j], dst_ref=(recv1, recv2)[tick][c].at[j],
            send_sem=z_send.at[j], recv_sem=z_recv.at[tick, c],
            device_id={"graph": dests[j]}, device_id_type=MESH,
        )

    loads[0].wait()
    for c in range(NC):
        for j in ORDER:
            @pl.when(has_dest[j])
            def _():
                if c == 0:
                    want_copy(j).wait_recv()
                stage1[c][j] = state_v[wants_in[j, j], :, cols(c)]

                @pl.when(odd)
                def _():
                    block_copy(0, j, c).start()

    for j in ORDER:
        @pl.when(jnp.logical_not(has_source[j]))
        def _():
            for c in range(NC):
                recv1[c][j] = jnp.zeros((BLK, WIDTHS[c]), F32)
                recv2[c][j] = jnp.zeros((BLK, WIDTHS[c]), F32)

    loads[1].wait()
    loads[4].wait()
    loads[5].wait()

    def build(b, carry):
        for s in range(NB + NJ):
            tile = jnp.zeros((BLK, BLK), F32)
            for k in range(KMAX):
                live = ((slot[b, k] == s) & (k < count[b])).astype(jnp.int32)
                tile += live.astype(F32) * vals_v[b, k]
            hi, lo = split(0.9 * tile)
            rows = pl.ds(pl.multiple_of(b * BLK, BLK), BLK)
            a_hi[rows, pl.ds(s * BLK, BLK)] = hi
            a_lo[rows, pl.ds(s * BLK, BLK)] = lo
        return carry

    lax.fori_loop(0, NB, build, 0)

    beta = jnp.float32(0.0)
    for s in range(n_seg):
        beta = jnp.where(sec == s, jnp.float32(math.log(0.5 / (s + 1.0) + 1.0)), beta)
    loads[2].wait()

    def fold(i, carry):
        rows = pl.ds(pl.multiple_of(i * BLK, BLK), BLK)
        r = lax.broadcasted_iota(jnp.int32, (BLK, D), 0) + i * BLK
        q = lax.broadcasted_iota(jnp.int32, (BLK, D), 1)
        w = beta * w_v[rows, :] + jnp.where(r == q, 1.0 - beta, 0.0)
        w_hi[rows, :], w_lo[rows, :] = split(w)
        return carry

    lax.fori_loop(0, D // BLK, fold, 0)

    def aggregate(lo_col, feats):
        k = pl.ds(lo_col, NB * BLK)
        return adjacent(a_hi[:, k], a_lo[:, k], feats)

    def own_part(feats, first_feats, c):
        z[c][...] = aggregate(0, feats) + 0.1 * first_feats

    def arrive(tick, c):
        ref = (recv1, recv2)[tick][c]
        for blocks_due in range(2, NJ + 1):
            @pl.when(due == blocks_due)
            def _():
                due_ref = ref.at[pl.ds(0, blocks_due)]
                pltpu.make_async_copy(due_ref, due_ref, z_recv.at[tick, c]).wait()

    def rest_part(tick, c, finish):
        arrive(tick, c)
        recv = (recv1, recv2)[tick][c]
        if tick == 0 and c == GO:
            @pl.when(odd)
            def _():
                pl.semaphore_signal(go_sem, inc=1, device_id={"segment": sec - 1}, device_id_type=MESH)
        zc = split(z[c][...] + aggregate(V, recv[...].reshape(V, WIDTHS[c])))
        for n in range(NC):
            part_n = weighted(zc, w_hi[cols(c), cols(n)], w_lo[cols(c), cols(n)])
            if c > 0:
                part_n += acc[:, cols(n)]
            if c < NC - 1:
                acc[:, cols(n)] = part_n
            else:
                finish(n, jnp.maximum(part_n, 0.0))

    loads[3].wait()
    for c in range(NC):
        own_part(state_v[:, :, cols(c)].reshape(V, WIDTHS[c]), init_v[:, :, cols(c)].reshape(V, WIDTHS[c]), c)

    def hand_copy(n):
        return pltpu.make_async_remote_copy(
            src_ref=handed.at[:, :, cols(n)], dst_ref=h_in[n], send_sem=x_send, recv_sem=h_recv.at[n],
            device_id={"segment": sec + 1}, device_id_type=MESH,
        )

    def finish_first(n, value):
        handed[:, :, cols(n)] = value.reshape(NB, BLK, WIDTHS[n])

        @pl.when(jnp.logical_not(last))
        def _():
            hand_copy(n).start()

    @pl.when(jnp.logical_not(odd))
    def _():
        pl.semaphore_wait(go_sem, 1)
        for c in range(NC):
            for j in ORDER:
                @pl.when(has_dest[j])
                def _():
                    block_copy(0, j, c).start()

    def forward(c):
        pltpu.make_async_copy(h_in[c], h_in[c], h_recv.at[c]).wait()
        for j in ORDER:
            @pl.when(has_dest[j])
            def _():
                stage2[c][j] = h_in[c][wants_in[j, j]]
                block_copy(1, j, c).start()

    def early(c):
        @pl.when(jnp.logical_not(odd))
        def _():
            forward(c)

    for c in range(NC):
        rest_part(0, c, finish_first)
        if c == 0:
            early(0)
        if c == 2:
            early(1)

    @pl.when(odd)
    def _():
        forward(0)
        forward(1)
    for c in range(2, NC):
        forward(c)

    pltpu.make_async_copy(init_in, init_in, init_recv).wait()
    for c in range(NC):
        own_part(h_in[c][...].reshape(V, WIDTHS[c]), init_in[:, :, cols(c)].reshape(V, WIDTHS[c]), c)
    for c in range(NC - 1):
        rest_part(1, c, None)
    z_last[...] = z[NC - 1][...]
    arrive(1, NC - 1)

    for j in range(NJ):
        @pl.when(has_source[j])
        def _():
            want_copy(j).wait_send()

        @pl.when(has_dest[j])
        def _():
            sent = w_v.at[pl.ds(0, 2 * BLK)]
            pltpu.make_async_copy(sent, sent, z_send.at[j]).wait()

    @pl.when(jnp.logical_not(last))
    def _():
        pltpu.make_async_copy(w_v, w_v, x_send).wait()


def finish_kernel(handed, acc, z_last, recv_last, a_hi, a_lo, w_hi, w_lo, handed_out, advanced_out, result, sem):
    last = NC - 1
    store = pltpu.make_async_copy(handed, handed_out, sem.at[NC])
    store.start()
    k = pl.ds(V, NJ * BLK)
    feats = recv_last[...].reshape(V, WIDTHS[last])
    parts = split(z_last[...] + adjacent(a_hi[:, k], a_lo[:, k], feats))

    def store_part(n):
        return pltpu.make_async_copy(result.at[:, :, cols(n)], advanced_out.at[:, :, cols(n)], sem.at[n])

    for n in range(NC):
        value = acc[:, cols(n)] + weighted(parts, w_hi[cols(last), cols(n)], w_lo[cols(last), cols(n)])
        result[:, :, cols(n)] = jnp.maximum(value, 0.0).reshape(NB, BLK, WIDTHS[n])
        store_part(n).start()
    store.wait()
    for n in range(NC):
        store_part(n).wait()


def blocks(x):
    return x.reshape(NB, BLK, D)


def shards(n_seg, n_graph, state, initial, fresh, weights, wants, adj_slot, adj_count, adj_vals):
    hbm = pl.BlockSpec(memory_space=pltpu.HBM)
    vmem = pl.BlockSpec(memory_space=pltpu.VMEM)
    dma = pltpu.SemaphoreType.DMA
    carried = (
        pltpu.VMEM((NB, BLK, D), F32),
        pltpu.VMEM((V, D), F32),
        pltpu.VMEM((V, WIDTHS[-1]), F32),
        pltpu.VMEM((NJ, BLK, WIDTHS[-1]), F32),
        pltpu.VMEM((V, (NB + NJ) * BLK), BF16),
        pltpu.VMEM((V, (NB + NJ) * BLK), BF16),
        pltpu.VMEM((D, D), BF16),
        pltpu.VMEM((D, D), BF16),
    )
    results = pl.pallas_call(
        functools.partial(kernel, n_seg, n_graph),
        out_shape=carried,
        in_specs=[hbm] * 8,
        out_specs=(vmem,) * len(carried),
        scratch_shapes=[
            pltpu.VMEM((NB, BLK, D), F32),
            pltpu.VMEM((NB, KMAX, BLK, BLK), F32),
            pltpu.VMEM((D, D), F32),
            pltpu.VMEM((NB, BLK, D), F32),
            pltpu.VMEM((NB, BLK, D), F32),
            pltpu.SMEM((NJ, NJ), jnp.int32),
            pltpu.SMEM((NB, KMAX), jnp.int32),
            pltpu.SMEM((NB,), jnp.int32),
        ]
        + [pltpu.VMEM((NB, BLK, w), F32) for _ in range(5) for w in WIDTHS]
        + [pltpu.VMEM((V, w), F32) for w in WIDTHS]
        + [
            dma((6,)), dma((NJ,)), dma((NJ,)), dma((NJ,)), dma((2, NC)), dma, dma((NC,)), dma,
            pltpu.SemaphoreType.REGULAR,
        ],
        compiler_params=pltpu.CompilerParams(
            collective_id=0, has_side_effects=True, vmem_limit_bytes=40 * 1024 * 1024
        ),
    )(
        *(
            pltpu.with_memory_space_constraint(x, pltpu.HBM)
            for x in (
                adj_slot, adj_count, blocks(state), blocks(initial), blocks(fresh), weights[0], adj_vals,
                wants.reshape(NJ),
            )
        )
    )
    out = pltpu.HBM((NB, BLK, D), F32)
    handed, advanced = pl.pallas_call(
        finish_kernel,
        out_shape=(out, out),
        in_specs=[vmem] * len(carried),
        out_specs=(hbm, hbm),
        scratch_shapes=[pltpu.VMEM((NB, BLK, D), F32), dma((NC + 1,))],
        compiler_params=pltpu.CompilerParams(vmem_limit_bytes=20 * 1024 * 1024),
    )(*results)
    return handed.reshape(1, V, D), advanced.reshape(1, V, D)


def solution(mesh):
    return jax.shard_map(
        functools.partial(shards, mesh.shape["segment"], mesh.shape["graph"]),
        mesh=mesh,
        in_specs=(
            P("segment", "graph", None),
            P("segment", "graph", None),
            P("graph", None),
            P("segment", None, None),
            P("graph", None, None),
            P("graph", None),
            P("graph"),
            P("graph", None, None, None),
        ),
        out_specs=(P("segment", "graph", None), P("segment", "graph", None)),
        check_vma=False,
    )
```

```python
import functools
import math

import jax
import jax.numpy as jnp
from jax import lax
from jax.experimental import pallas as pl
from jax.experimental.pallas import tpu as pltpu
from jax.sharding import PartitionSpec as P

MESH = pl.DeviceIdType.MESH
F32 = jnp.float32
BF16 = jnp.bfloat16
D = 1024
BLK = 128
NB = 4
KMAX = 4
V = NB * BLK
OFFSETS = (1, -1, 2, -2)
NJ = len(OFFSETS)
WIDTHS = (256, 256, 256, 128, 128)
NC = len(WIDTHS)
STARTS = tuple(sum(WIDTHS[:c]) for c in range(NC))
ORDER = (0, 1, 2, 3)
GO = 2


def split(x):
    hi = x.astype(BF16)
    return hi, (x - hi.astype(F32)).astype(BF16)


def dot(a, b):
    return jnp.dot(a, b, preferred_element_type=F32)


def adjacent(a_hi, a_lo, feats):
    hi, lo = split(feats)
    width = feats.shape[1]
    if width > BLK:
        return dot(a_hi, hi) + dot(a_lo, hi) + dot(a_hi, lo)
    both = dot(a_hi, jnp.concatenate([hi, lo], axis=1))
    return both[:, :width] + both[:, width:] + dot(a_lo, hi)


def weighted(parts, w_hi, w_lo):
    hi, lo = parts
    if hi.shape[1] > BLK:
        return dot(hi, w_hi) + dot(lo, w_hi) + dot(hi, w_lo)
    return dot(jnp.concatenate([hi, lo], axis=1), jnp.concatenate([w_hi, w_hi], axis=0)) + dot(hi, w_lo)


def cols(c):
    return pl.ds(STARTS[c], WIDTHS[c])


def kernel(
    n_seg, n_graph,
    slot_hbm, count_hbm, state, initial, fresh, weights, vals, wants_hbm,
    handed, acc, z_last, recv_last, a_hi, a_lo, w_hi, w_lo,
    state_v, vals_v, w_v, init_v, init_in, wants_in, slot, count, wants, *rest,
):
    h_in, stage1, stage2, recv1, recv2, z = (rest[i * NC : (i + 1) * NC] for i in range(6))
    recv2 = recv2[: NC - 1] + (recv_last,)
    (load_sem, want_send, want_recv, z_send, z_recv, x_send, h_recv, init_recv, go_sem) = rest[6 * NC :]
    sec = lax.axis_index("segment")
    part = lax.axis_index("graph")
    first, last = sec == 0, sec == n_seg - 1
    odd = sec % 2 == 1
    dests = [part + o for o in OFFSETS]
    sources = [part - o for o in OFFSETS]
    has_dest = [(d >= 0) & (d < n_graph) for d in dests]
    has_source = [(d >= 0) & (d < n_graph) for d in sources]

    due = sum(ok.astype(jnp.int32) for ok in has_source)

    loads = [
        pltpu.make_async_copy(src, dst, load_sem.at[i])
        for i, (src, dst) in enumerate(
            ((state, state_v), (vals, vals_v), (weights, w_v), (initial, init_v), (slot_hbm, slot), (count_hbm, count), (wants_hbm, wants))
        )
    ]
    loads[6].start()
    loads[0].start()

    barrier = pltpu.get_barrier_semaphore()
    expected = jnp.int32(0)
    for d, ok in zip(dests, has_dest):
        @pl.when(ok)
        def _():
            pl.semaphore_signal(barrier, inc=1, device_id={"graph": d}, device_id_type=MESH)
        expected += ok.astype(jnp.int32)

    @pl.when(jnp.logical_not(last))
    def _():
        pl.semaphore_signal(barrier, inc=1, device_id={"segment": sec + 1}, device_id_type=MESH)

    @pl.when(jnp.logical_not(first))
    def _():
        pl.semaphore_signal(barrier, inc=1, device_id={"segment": sec - 1}, device_id_type=MESH)

    expected += jnp.logical_not(last).astype(jnp.int32) + jnp.logical_not(first).astype(jnp.int32)
    pl.semaphore_wait(barrier, expected)

    def want_copy(j):
        return pltpu.make_async_remote_copy(
            src_ref=wants, dst_ref=wants_in.at[j], send_sem=want_send.at[j], recv_sem=want_recv.at[j],
            device_id={"graph": sources[j]}, device_id_type=MESH,
        )

    def init_copy():
        return pltpu.make_async_remote_copy(
            src_ref=initial, dst_ref=init_in, send_sem=x_send, recv_sem=init_recv,
            device_id={"segment": sec + 1}, device_id_type=MESH,
        )

    loads[6].wait()
    for j in ORDER:
        @pl.when(has_source[j])
        def _():
            want_copy(j).start()

    for load in loads[1:6]:
        load.start()

    @pl.when(jnp.logical_not(last))
    def _():
        init_copy().start()

    @pl.when(first)
    def _():
        pltpu.make_async_copy(fresh, init_in, init_recv).start()
        for c in range(NC):
            pltpu.make_async_copy(fresh.at[:, :, cols(c)], h_in[c], h_recv.at[c]).start()

    def block_copy(tick, j, c):
        return pltpu.make_async_remote_copy(
            src_ref=(stage1, stage2)[tick][c].at[j], dst_ref=(recv1, recv2)[tick][c].at[j],
            send_sem=z_send.at[j], recv_sem=z_recv.at[tick, c],
            device_id={"graph": dests[j]}, device_id_type=MESH,
        )

    loads[0].wait()
    for c in range(NC):
        for j in ORDER:
            @pl.when(has_dest[j])
            def _():
                if c == 0:
                    want_copy(j).wait_recv()
                stage1[c][j] = state_v[wants_in[j, j], :, cols(c)]

                @pl.when(odd)
                def _():
                    block_copy(0, j, c).start()

    for j in ORDER:
        @pl.when(jnp.logical_not(has_source[j]))
        def _():
            for c in range(NC):
                recv1[c][j] = jnp.zeros((BLK, WIDTHS[c]), F32)
                recv2[c][j] = jnp.zeros((BLK, WIDTHS[c]), F32)

    loads[1].wait()
    loads[4].wait()
    loads[5].wait()

    def build(b, carry):
        for s in range(NB + NJ):
            tile = jnp.zeros((BLK, BLK), F32)
            for k in range(KMAX):
                live = ((slot[b, k] == s) & (k < count[b])).astype(jnp.int32)
                tile += live.astype(F32) * vals_v[b, k]
            hi, lo = split(0.9 * tile)
            rows = pl.ds(pl.multiple_of(b * BLK, BLK), BLK)
            a_hi[rows, pl.ds(s * BLK, BLK)] = hi
            a_lo[rows, pl.ds(s * BLK, BLK)] = lo
        return carry

    lax.fori_loop(0, NB, build, 0)

    beta = jnp.float32(0.0)
    for s in range(n_seg):
        beta = jnp.where(sec == s, jnp.float32(math.log(0.5 / (s + 1.0) + 1.0)), beta)
    loads[2].wait()

    def fold(i, carry):
        rows = pl.ds(pl.multiple_of(i * BLK, BLK), BLK)
        r = lax.broadcasted_iota(jnp.int32, (BLK, D), 0) + i * BLK
        q = lax.broadcasted_iota(jnp.int32, (BLK, D), 1)
        w = beta * w_v[rows, :] + jnp.where(r == q, 1.0 - beta, 0.0)
        w_hi[rows, :], w_lo[rows, :] = split(w)
        return carry

    lax.fori_loop(0, D // BLK, fold, 0)

    def aggregate(lo_col, feats):
        k = pl.ds(lo_col, NB * BLK)
        return adjacent(a_hi[:, k], a_lo[:, k], feats)

    def own_part(feats, first_feats, c):
        z[c][...] = aggregate(0, feats) + 0.1 * first_feats

    def arrive(tick, c):
        ref = (recv1, recv2)[tick][c]
        for blocks_due in range(2, NJ + 1):
            @pl.when(due == blocks_due)
            def _():
                due_ref = ref.at[pl.ds(0, blocks_due)]
                pltpu.make_async_copy(due_ref, due_ref, z_recv.at[tick, c]).wait()

    def rest_part(tick, c, finish):
        arrive(tick, c)
        recv = (recv1, recv2)[tick][c]
        if tick == 0 and c == GO:
            @pl.when(odd)
            def _():
                pl.semaphore_signal(go_sem, inc=1, device_id={"segment": sec - 1}, device_id_type=MESH)
        zc = split(z[c][...] + aggregate(V, recv[...].reshape(V, WIDTHS[c])))
        for n in range(NC):
            part_n = weighted(zc, w_hi[cols(c), cols(n)], w_lo[cols(c), cols(n)])
            if c > 0:
                part_n += acc[:, cols(n)]
            if c < NC - 1:
                acc[:, cols(n)] = part_n
            else:
                finish(n, jnp.maximum(part_n, 0.0))

    loads[3].wait()
    for c in range(NC):
        own_part(state_v[:, :, cols(c)].reshape(V, WIDTHS[c]), init_v[:, :, cols(c)].reshape(V, WIDTHS[c]), c)

    def hand_copy(n):
        return pltpu.make_async_remote_copy(
            src_ref=handed.at[:, :, cols(n)], dst_ref=h_in[n], send_sem=x_send, recv_sem=h_recv.at[n],
            device_id={"segment": sec + 1}, device_id_type=MESH,
        )

    def finish_first(n, value):
        handed[:, :, cols(n)] = value.reshape(NB, BLK, WIDTHS[n])

        @pl.when(jnp.logical_not(last))
        def _():
            hand_copy(n).start()

    @pl.when(jnp.logical_not(odd))
    def _():
        pl.semaphore_wait(go_sem, 1)
        for c in range(NC):
            for j in ORDER:
                @pl.when(has_dest[j])
                def _():
                    block_copy(0, j, c).start()

    def forward(c):
        pltpu.make_async_copy(h_in[c], h_in[c], h_recv.at[c]).wait()
        for j in ORDER:
            @pl.when(has_dest[j])
            def _():
                stage2[c][j] = h_in[c][wants_in[j, j]]
                block_copy(1, j, c).start()

    def early(c):
        @pl.when(jnp.logical_not(odd))
        def _():
            forward(c)

    for c in range(NC):
        rest_part(0, c, finish_first)
        if c == 0:
            early(0)
        if c == 2:
            early(1)

    @pl.when(odd)
    def _():
        forward(0)
        forward(1)
    for c in range(2, NC):
        forward(c)

    pltpu.make_async_copy(init_in, init_in, init_recv).wait()
    for c in range(NC):
        own_part(h_in[c][...].reshape(V, WIDTHS[c]), init_in[:, :, cols(c)].reshape(V, WIDTHS[c]), c)
    for c in range(NC - 1):
        rest_part(1, c, None)
    z_last[...] = z[NC - 1][...]
    arrive(1, NC - 1)

    for j in range(NJ):
        @pl.when(has_source[j])
        def _():
            want_copy(j).wait_send()

        @pl.when(has_dest[j])
        def _():
            sent = w_v.at[pl.ds(0, 2 * BLK)]
            pltpu.make_async_copy(sent, sent, z_send.at[j]).wait()

    @pl.when(jnp.logical_not(last))
    def _():
        pltpu.make_async_copy(w_v, w_v, x_send).wait()


def finish_kernel(handed, acc, z_last, recv_last, a_hi, a_lo, w_hi, w_lo, handed_out, advanced_out, result, sem):
    last = NC - 1
    store = pltpu.make_async_copy(handed, handed_out, sem.at[NC])
    store.start()
    k = pl.ds(V, NJ * BLK)
    feats = recv_last[...].reshape(V, WIDTHS[last])
    parts = split(z_last[...] + adjacent(a_hi[:, k], a_lo[:, k], feats))

    def store_part(n):
        return pltpu.make_async_copy(result.at[:, :, cols(n)], advanced_out.at[:, :, cols(n)], sem.at[n])

    for n in range(NC):
        value = acc[:, cols(n)] + weighted(parts, w_hi[cols(last), cols(n)], w_lo[cols(last), cols(n)])
        result[:, :, cols(n)] = jnp.maximum(value, 0.0).reshape(NB, BLK, WIDTHS[n])
        store_part(n).start()
    store.wait()
    for n in range(NC):
        store_part(n).wait()


def blocks(x):
    return x.reshape(NB, BLK, D)


def shards(n_seg, n_graph, state, initial, fresh, weights, wants, adj_slot, adj_count, adj_vals):
    hbm = pl.BlockSpec(memory_space=pltpu.HBM)
    vmem = pl.BlockSpec(memory_space=pltpu.VMEM)
    dma = pltpu.SemaphoreType.DMA
    carried = (
        pltpu.VMEM((NB, BLK, D), F32),
        pltpu.VMEM((V, D), F32),
        pltpu.VMEM((V, WIDTHS[-1]), F32),
        pltpu.VMEM((NJ, BLK, WIDTHS[-1]), F32),
        pltpu.VMEM((V, (NB + NJ) * BLK), BF16),
        pltpu.VMEM((V, (NB + NJ) * BLK), BF16),
        pltpu.VMEM((D, D), BF16),
        pltpu.VMEM((D, D), BF16),
    )
    results = pl.pallas_call(
        functools.partial(kernel, n_seg, n_graph),
        out_shape=carried,
        in_specs=[hbm] * 8,
        out_specs=(vmem,) * len(carried),
        scratch_shapes=[
            pltpu.VMEM((NB, BLK, D), F32),
            pltpu.VMEM((NB, KMAX, BLK, BLK), F32),
            pltpu.VMEM((D, D), F32),
            pltpu.VMEM((NB, BLK, D), F32),
            pltpu.VMEM((NB, BLK, D), F32),
            pltpu.SMEM((NJ, NJ), jnp.int32),
            pltpu.SMEM((NB, KMAX), jnp.int32),
            pltpu.SMEM((NB,), jnp.int32),
            pltpu.SMEM((NJ,), jnp.int32),
        ]
        + [pltpu.VMEM((NB, BLK, w), F32) for _ in range(5) for w in WIDTHS]
        + [pltpu.VMEM((V, w), F32) for w in WIDTHS]
        + [
            dma((7,)), dma((NJ,)), dma((NJ,)), dma((NJ,)), dma((2, NC)), dma, dma((NC,)), dma,
            pltpu.SemaphoreType.REGULAR,
        ],
        compiler_params=pltpu.CompilerParams(
            collective_id=0, has_side_effects=True, vmem_limit_bytes=40 * 1024 * 1024
        ),
    )(
        *(
            pltpu.with_memory_space_constraint(x, pltpu.HBM)
            for x in (
                adj_slot, adj_count, blocks(state), blocks(initial), blocks(fresh), weights[0], adj_vals,
                wants.reshape(NJ),
            )
        )
    )
    out = pltpu.HBM((NB, BLK, D), F32)
    handed, advanced = pl.pallas_call(
        finish_kernel,
        out_shape=(out, out),
        in_specs=[vmem] * len(carried),
        out_specs=(hbm, hbm),
        scratch_shapes=[pltpu.VMEM((NB, BLK, D), F32), dma((NC + 1,))],
        compiler_params=pltpu.CompilerParams(vmem_limit_bytes=20 * 1024 * 1024),
    )(*results)
    return handed.reshape(1, V, D), advanced.reshape(1, V, D)


def solution(mesh):
    return jax.shard_map(
        functools.partial(shards, mesh.shape["segment"], mesh.shape["graph"]),
        mesh=mesh,
        in_specs=(
            P("segment", "graph", None),
            P("segment", "graph", None),
            P("graph", None),
            P("segment", None, None),
            P("graph", None, None),
            P("graph", None),
            P("graph"),
            P("graph", None, None, None),
        ),
        out_specs=(P("segment", "graph", None), P("segment", "graph", None)),
        check_vma=False,
    )
```

```python
import functools
import math

import jax
import jax.numpy as jnp
from jax import lax
from jax.experimental import pallas as pl
from jax.experimental.pallas import tpu as pltpu
from jax.sharding import PartitionSpec as P

MESH = pl.DeviceIdType.MESH
F32 = jnp.float32
BF16 = jnp.bfloat16
D = 1024
BLK = 128
NB = 4
KMAX = 4
V = NB * BLK
OFFSETS = (1, -1, 2, -2)
NJ = len(OFFSETS)
WIDTHS = (256, 256, 256, 128, 128)
NC = len(WIDTHS)
STARTS = tuple(sum(WIDTHS[:c]) for c in range(NC))
ORDER = (0, 1, 2, 3)
GO = 2


def split(x):
    hi = x.astype(BF16)
    return hi, (x - hi.astype(F32)).astype(BF16)


def dot(a, b):
    return jnp.dot(a, b, preferred_element_type=F32)


def adjacent(a_hi, a_lo, feats):
    hi, lo = split(feats)
    width = feats.shape[1]
    if width > BLK:
        return dot(a_hi, hi) + dot(a_lo, hi) + dot(a_hi, lo)
    both = dot(a_hi, jnp.concatenate([hi, lo], axis=1))
    return both[:, :width] + both[:, width:] + dot(a_lo, hi)


def weighted(parts, w_hi, w_lo):
    hi, lo = parts
    if hi.shape[1] > BLK:
        return dot(hi, w_hi) + dot(lo, w_hi) + dot(hi, w_lo)
    return dot(jnp.concatenate([hi, lo], axis=1), jnp.concatenate([w_hi, w_hi], axis=0)) + dot(hi, w_lo)


def cols(c):
    return pl.ds(STARTS[c], WIDTHS[c])


def kernel(
    n_seg, n_graph,
    slot_hbm, count_hbm, state, initial, fresh, weights, vals, wants_hbm,
    handed, acc, z_last, recv_last, a_hi, a_lo, w_hi, w_lo,
    state_v, vals_v, w_v, init_v, init_in, wants_in, slot, count, wants, *rest,
):
    h_in, stage1, stage2, recv1, recv2, z = (rest[i * NC : (i + 1) * NC] for i in range(6))
    recv2 = recv2[: NC - 1] + (recv_last,)
    (load_sem, want_send, want_recv, z_send, z_recv, x_send, h_recv, init_recv, go_sem) = rest[6 * NC :]
    sec = lax.axis_index("segment")
    part = lax.axis_index("graph")
    first, last = sec == 0, sec == n_seg - 1
    odd = sec % 2 == 1
    dests = [part + o for o in OFFSETS]
    sources = [part - o for o in OFFSETS]
    has_dest = [(d >= 0) & (d < n_graph) for d in dests]
    has_source = [(d >= 0) & (d < n_graph) for d in sources]

    due = sum(ok.astype(jnp.int32) for ok in has_source)

    loads = [
        pltpu.make_async_copy(src, dst, load_sem.at[i])
        for i, (src, dst) in enumerate(
            ((state, state_v), (vals, vals_v), (weights, w_v), (initial, init_v), (slot_hbm, slot), (count_hbm, count), (wants_hbm, wants))
        )
    ]
    loads[6].start()
    loads[0].start()

    barrier = pltpu.get_barrier_semaphore()
    expected = jnp.int32(0)
    for d, ok in zip(dests, has_dest):
        @pl.when(ok)
        def _():
            pl.semaphore_signal(barrier, inc=1, device_id={"graph": d}, device_id_type=MESH)
        expected += ok.astype(jnp.int32)

    @pl.when(jnp.logical_not(last))
    def _():
        pl.semaphore_signal(barrier, inc=1, device_id={"segment": sec + 1}, device_id_type=MESH)

    @pl.when(jnp.logical_not(first))
    def _():
        pl.semaphore_signal(barrier, inc=1, device_id={"segment": sec - 1}, device_id_type=MESH)

    expected += jnp.logical_not(last).astype(jnp.int32) + jnp.logical_not(first).astype(jnp.int32)
    pl.semaphore_wait(barrier, expected)

    def want_copy(j):
        return pltpu.make_async_remote_copy(
            src_ref=wants, dst_ref=wants_in.at[j], send_sem=want_send.at[j], recv_sem=want_recv.at[j],
            device_id={"graph": sources[j]}, device_id_type=MESH,
        )

    def init_copy():
        return pltpu.make_async_remote_copy(
            src_ref=initial, dst_ref=init_in, send_sem=x_send, recv_sem=init_recv,
            device_id={"segment": sec + 1}, device_id_type=MESH,
        )

    loads[6].wait()
    for j in ORDER:
        @pl.when(has_source[j])
        def _():
            want_copy(j).start()

    for load in loads[1:6]:
        load.start()

    @pl.when(jnp.logical_not(last))
    def _():
        init_copy().start()

    @pl.when(first)
    def _():
        pltpu.make_async_copy(fresh, init_in, init_recv).start()
        for c in range(NC):
            pltpu.make_async_copy(fresh.at[:, :, cols(c)], h_in[c], h_recv.at[c]).start()

    def block_copy(tick, j, c):
        return pltpu.make_async_remote_copy(
            src_ref=(stage1, stage2)[tick][c].at[j], dst_ref=(recv1, recv2)[tick][c].at[j],
            send_sem=z_send.at[j], recv_sem=z_recv.at[tick, c],
            device_id={"graph": dests[j]}, device_id_type=MESH,
        )

    loads[0].wait()
    for c in range(NC):
        for j in ORDER:
            @pl.when(has_dest[j])
            def _():
                if c == 0:
                    want_copy(j).wait_recv()
                stage1[c][j] = state_v[wants_in[j, j], :, cols(c)]

                @pl.when(odd)
                def _():
                    block_copy(0, j, c).start()

    for j in ORDER:
        @pl.when(jnp.logical_not(has_source[j]))
        def _():
            for c in range(NC):
                recv1[c][j] = jnp.zeros((BLK, WIDTHS[c]), F32)
                recv2[c][j] = jnp.zeros((BLK, WIDTHS[c]), F32)

    loads[1].wait()
    loads[4].wait()
    loads[5].wait()

    def build(b, carry):
        for s in range(NB + NJ):
            tile = jnp.zeros((BLK, BLK), F32)
            for k in range(KMAX):
                live = ((slot[b, k] == s) & (k < count[b])).astype(jnp.int32)
                tile += live.astype(F32) * vals_v[b, k]
            hi, lo = split(0.9 * tile)
            rows = pl.ds(pl.multiple_of(b * BLK, BLK), BLK)
            a_hi[rows, pl.ds(s * BLK, BLK)] = hi
            a_lo[rows, pl.ds(s * BLK, BLK)] = lo
        return carry

    lax.fori_loop(0, NB, build, 0)

    beta = jnp.float32(0.0)
    for s in range(n_seg):
        beta = jnp.where(sec == s, jnp.float32(math.log(0.5 / (s + 1.0) + 1.0)), beta)
    loads[2].wait()

    def fold(i, carry):
        rows = pl.ds(pl.multiple_of(i * BLK, BLK), BLK)
        r = lax.broadcasted_iota(jnp.int32, (BLK, D), 0) + i * BLK
        q = lax.broadcasted_iota(jnp.int32, (BLK, D), 1)
        w = beta * w_v[rows, :] + jnp.where(r == q, 1.0 - beta, 0.0)
        w_hi[rows, :], w_lo[rows, :] = split(w)
        return carry

    lax.fori_loop(0, D // BLK, fold, 0)

    def aggregate(lo_col, feats):
        k = pl.ds(lo_col, NB * BLK)
        return adjacent(a_hi[:, k], a_lo[:, k], feats)

    def own_part(feats, first_feats, c):
        z[c][...] = aggregate(0, feats) + 0.1 * first_feats

    def arrive(tick, c):
        ref = (recv1, recv2)[tick][c]
        for blocks_due in range(2, NJ + 1):
            @pl.when(due == blocks_due)
            def _():
                due_ref = ref.at[pl.ds(0, blocks_due)]
                pltpu.make_async_copy(due_ref, due_ref, z_recv.at[tick, c]).wait()

    def rest_part(tick, c, finish):
        arrive(tick, c)
        recv = (recv1, recv2)[tick][c]
        if tick == 0 and c == GO:
            @pl.when(odd)
            def _():
                pl.semaphore_signal(go_sem, inc=1, device_id={"segment": sec - 1}, device_id_type=MESH)
        zc = split(z[c][...] + aggregate(V, recv[...].reshape(V, WIDTHS[c])))
        for n in range(NC):
            part_n = weighted(zc, w_hi[cols(c), cols(n)], w_lo[cols(c), cols(n)])
            if c > 0:
                part_n += acc[:, cols(n)]
            if c < NC - 1:
                acc[:, cols(n)] = part_n
            else:
                finish(n, jnp.maximum(part_n, 0.0))

    loads[3].wait()
    for c in range(NC):
        own_part(state_v[:, :, cols(c)].reshape(V, WIDTHS[c]), init_v[:, :, cols(c)].reshape(V, WIDTHS[c]), c)

    def hand_copy(n):
        return pltpu.make_async_remote_copy(
            src_ref=handed.at[:, :, cols(n)], dst_ref=h_in[n], send_sem=x_send, recv_sem=h_recv.at[n],
            device_id={"segment": sec + 1}, device_id_type=MESH,
        )

    def finish_first(n, value):
        handed[:, :, cols(n)] = value.reshape(NB, BLK, WIDTHS[n])

        @pl.when(jnp.logical_not(last))
        def _():
            hand_copy(n).start()

    @pl.when(jnp.logical_not(odd))
    def _():
        pl.semaphore_wait(go_sem, 1)
        for c in range(NC):
            for j in ORDER:
                @pl.when(has_dest[j])
                def _():
                    block_copy(0, j, c).start()

    def forward(c):
        pltpu.make_async_copy(h_in[c], h_in[c], h_recv.at[c]).wait()
        for j in ORDER:
            @pl.when(has_dest[j])
            def _():
                stage2[c][j] = h_in[c][wants_in[j, j]]
                block_copy(1, j, c).start()

    def early(c):
        @pl.when(jnp.logical_not(odd))
        def _():
            forward(c)

    for c in range(NC):
        rest_part(0, c, finish_first)
        if c == 0:
            early(0)
        if c == 2:
            early(1)

    @pl.when(odd)
    def _():
        forward(0)
        forward(1)
    for c in range(2, NC):
        forward(c)

    pltpu.make_async_copy(init_in, init_in, init_recv).wait()
    for c in range(NC):
        own_part(h_in[c][...].reshape(V, WIDTHS[c]), init_in[:, :, cols(c)].reshape(V, WIDTHS[c]), c)
    for c in range(NC - 1):
        rest_part(1, c, None)
    z_last[...] = z[NC - 1][...]
    arrive(1, NC - 1)

    for j in range(NJ):
        @pl.when(has_source[j])
        def _():
            want_copy(j).wait_send()

        @pl.when(has_dest[j])
        def _():
            sent = w_v.at[pl.ds(0, 2 * BLK)]
            pltpu.make_async_copy(sent, sent, z_send.at[j]).wait()

    @pl.when(jnp.logical_not(last))
    def _():
        pltpu.make_async_copy(w_v, w_v, x_send).wait()


def finish_kernel(handed, acc, z_last, recv_last, a_hi, a_lo, w_hi, w_lo, handed_out, advanced_out, result, sem):
    last = NC - 1
    store = pltpu.make_async_copy(handed, handed_out, sem.at[NB])
    store.start()
    k = pl.ds(V, NJ * BLK)
    feats = recv_last[...].reshape(V, WIDTHS[last])
    parts = split(z_last[...] + adjacent(a_hi[:, k], a_lo[:, k], feats))

    def store_part(b):
        return pltpu.make_async_copy(result.at[b], advanced_out.at[b], sem.at[b])

    for b in range(NB):
        rows = slice(b * BLK, (b + 1) * BLK)
        value = acc[rows, :] + weighted([p[rows] for p in parts], w_hi[cols(last), :], w_lo[cols(last), :])
        result[b] = jnp.maximum(value, 0.0)
        store_part(b).start()
    store.wait()
    for b in range(NB):
        store_part(b).wait()


def blocks(x):
    return x.reshape(NB, BLK, D)


def shards(n_seg, n_graph, state, initial, fresh, weights, wants, adj_slot, adj_count, adj_vals):
    hbm = pl.BlockSpec(memory_space=pltpu.HBM)
    vmem = pl.BlockSpec(memory_space=pltpu.VMEM)
    dma = pltpu.SemaphoreType.DMA
    carried = (
        pltpu.VMEM((NB, BLK, D), F32),
        pltpu.VMEM((V, D), F32),
        pltpu.VMEM((V, WIDTHS[-1]), F32),
        pltpu.VMEM((NJ, BLK, WIDTHS[-1]), F32),
        pltpu.VMEM((V, (NB + NJ) * BLK), BF16),
        pltpu.VMEM((V, (NB + NJ) * BLK), BF16),
        pltpu.VMEM((D, D), BF16),
        pltpu.VMEM((D, D), BF16),
    )
    results = pl.pallas_call(
        functools.partial(kernel, n_seg, n_graph),
        out_shape=carried,
        in_specs=[hbm] * 8,
        out_specs=(vmem,) * len(carried),
        scratch_shapes=[
            pltpu.VMEM((NB, BLK, D), F32),
            pltpu.VMEM((NB, KMAX, BLK, BLK), F32),
            pltpu.VMEM((D, D), F32),
            pltpu.VMEM((NB, BLK, D), F32),
            pltpu.VMEM((NB, BLK, D), F32),
            pltpu.SMEM((NJ, NJ), jnp.int32),
            pltpu.SMEM((NB, KMAX), jnp.int32),
            pltpu.SMEM((NB,), jnp.int32),
            pltpu.SMEM((NJ,), jnp.int32),
        ]
        + [pltpu.VMEM((NB, BLK, w), F32) for _ in range(5) for w in WIDTHS]
        + [pltpu.VMEM((V, w), F32) for w in WIDTHS]
        + [
            dma((7,)), dma((NJ,)), dma((NJ,)), dma((NJ,)), dma((2, NC)), dma, dma((NC,)), dma,
            pltpu.SemaphoreType.REGULAR,
        ],
        compiler_params=pltpu.CompilerParams(
            collective_id=0, has_side_effects=True, vmem_limit_bytes=40 * 1024 * 1024
        ),
    )(
        *(
            pltpu.with_memory_space_constraint(x, pltpu.HBM)
            for x in (
                adj_slot, adj_count, blocks(state), blocks(initial), blocks(fresh), weights[0], adj_vals,
                wants.reshape(NJ),
            )
        )
    )
    out = pltpu.HBM((NB, BLK, D), F32)
    handed, advanced = pl.pallas_call(
        finish_kernel,
        out_shape=(out, out),
        in_specs=[vmem] * len(carried),
        out_specs=(hbm, hbm),
        scratch_shapes=[pltpu.VMEM((NB, BLK, D), F32), dma((NB + 1,))],
        compiler_params=pltpu.CompilerParams(vmem_limit_bytes=20 * 1024 * 1024),
    )(*results)
    return handed.reshape(1, V, D), advanced.reshape(1, V, D)


def solution(mesh):
    return jax.shard_map(
        functools.partial(shards, mesh.shape["segment"], mesh.shape["graph"]),
        mesh=mesh,
        in_specs=(
            P("segment", "graph", None),
            P("segment", "graph", None),
            P("graph", None),
            P("segment", None, None),
            P("graph", None, None),
            P("graph", None),
            P("graph"),
            P("graph", None, None, None),
        ),
        out_specs=(P("segment", "graph", None), P("segment", "graph", None)),
        check_vma=False,
    )
```
